32 devices in a mesh: subj: 2 (over x), row: 8 (over z, y), col: 2 (over core).
Axes of the slice: x: 2, y: 2, z: 4, core: 2. Of those that a mesh axis runs over, the one named last changes fastest.
Arguments:
- bold: bfloat16 [4, 256, 16, 16, 128], P('subj', None, 'row', 'col'), parts along dimension 0, may hold values from -6 to 6
- gm_index: int32 [16384], P(('row', 'col')), may hold values from -1 to 2047, as said below
- partners: int32 [128, 16], P(('row', 'col')), may hold values from -1 to 127, as said below
Outputs:
- connectome: bfloat16 [128, 16, 4, 128, 128], P(('row', 'col'), None, 'subj'), parts along dimension 2
The draws below stay inside these ranges and needn't reach their ends.
There are 2 independent parts, one for each index of `subj`. The reference program is written for one: setup_inputs(seed, part) draws one part's arguments, and reference() takes and returns one part's arrays. A program takes and returns all parts, laid end to end along the dimension named above; an argument that names none is the same for every part. Nothing has to cross between parts.
Inputs may be any that keep to these rules, and one draw needn't show every extreme that they name: `gm_index`: entries of one slab's 1024 rows are distinct voxel numbers, the last few of them -1; every slab has some -1 rows. `partners`: block g lies in slab g // 8, slabs numbered row-major over slab rows and columns. Slot 0 of block i names i, slot 1 names (i + 1) mod 128, slot 2 names (i - 1) mod 128; every named block lies in a slab whose slab row is within 2 of block i's slab row, counted cyclically. -1 marks an empty slot.
All inputs are finite; a program needn't handle non-finite values.
Results may differ from the reference program's by a relative error of at most 0.0053.
Values may be sent and summed in bfloat16 or wider, within the bound.
A program may use at most 128 MiB of HBM per device.

```python
import math
import jax
import jax.numpy as jnp
from jax import lax

W = 2
F = 256
BLOCK = 128
SX = 2
SY = 8
SZ = 128
K = 16
HOP = 2
GROUP = 16
NX = 16
NY = 16
NZ = 128
VLOC = 2048
ROWS_DEV = 1024
NBD = 8
NB = 128
N_ROW = 8
N_COL = 2


def draw_gm_index(key, part):
    slab_keys = jax.random.split(key, GROUP)

    def slab_rows(slab_key):
        first_key, second_key = jax.random.split(slab_key)
        shuffled = jax.random.permutation(first_key, VLOC).astype(jnp.int32)
        chosen = shuffled[:ROWS_DEV]
        spare = shuffled[ROWS_DEV]
        chosen = jnp.where(chosen == VLOC - 1, spare, chosen)
        chosen = chosen.at[0].set(VLOC - 1)
        padding = jax.random.randint(second_key, (), 1, BLOCK // 2 + 1)
        position = jnp.arange(ROWS_DEV).astype(jnp.int32)
        chosen = jnp.where(position >= ROWS_DEV - padding, -1, chosen)
        return chosen.astype(jnp.int32)
    return jax.vmap(slab_rows)(slab_keys).reshape(-1)


def draw_partners(key, part):
    row_key, col_key, block_key, empty_key = jax.random.split(key, 4)
    block_ids = jnp.arange(NB).astype(jnp.int32)
    home_row = block_ids // NBD // N_COL
    offsets = jax.random.randint(row_key, (NB, K), -HOP, HOP + 1)
    target_col = jax.random.randint(col_key, (NB, K), 0, N_COL)
    target_block = jax.random.randint(block_key, (NB, K), 0, NBD)
    target_row = (home_row[:, None] + offsets + N_ROW) % N_ROW
    named = (target_row * N_COL + target_col) * NBD + target_block
    empty = jax.random.randint(empty_key, (NB, K), 0, 4) == 0
    named = jnp.where(empty, -1, named)
    slot = jnp.arange(K).astype(jnp.int32)[None, :]
    named = jnp.where(slot == 0, block_ids[:, None], named)
    named = jnp.where(slot == 1, ((block_ids + 1) % NB)[:, None], named)
    named = jnp.where(slot == 2, ((block_ids - 1 + NB) % NB)[:, None], named)
    named = named.at[0, K - 1].set(-1)
    return named.astype(jnp.int32)


def shard_levels(key, shape, pieces, least, top_value):
    def one(dim, shards_of):
        steps = jax.random.uniform(jax.random.fold_in(jax.random.fold_in(key, 6), dim), (shards_of,), jnp.float32, least / len(pieces), top_value / len(pieces))
        return jnp.repeat(jnp.exp(steps), shape[dim] // shards_of).reshape((-1,) + (1,) * (len(shape) - dim - 1))

    gain = one(*pieces[0])
    for cut in pieces[1:]:
        gain = gain * one(*cut)
    return gain


def gaussian(rng, shape, width, most, shards=(), kind=jnp.bfloat16):
    entries = jax.random.normal(rng, shape, jnp.float32) * width
    if len(shards) > 0:
        entries = shard_levels(rng, shape, shards, -0.22, 0.18) * entries
    return jnp.clip(entries, min=-most, max=most).astype(kind)


def setup_inputs(seed: int = 0, part: int = 0) -> dict:
    seeds = jax.random.split(jax.random.key(seed), 4)
    own_keys = jax.random.split(jax.random.fold_in(seeds[3], part), 4)
    bold = gaussian(own_keys[0], (W, F, NX, NY, NZ), 1.0, 6.0, ((2, 8), (3, 2)))
    gm_index = draw_gm_index(jax.random.fold_in(seeds[3], 71), part)
    partners = draw_partners(jax.random.fold_in(seeds[3], 71), part)
    return dict(bold=bold, gm_index=gm_index, partners=partners)


side_weight = math.exp(-0.5) / (1.0 + 2.0 * math.exp(-0.5))
centre_weight = 1.0 / (1.0 + 2.0 * math.exp(-0.5))

def gaussian_blur(padded):
    first = side_weight * padded[:, :, :-2] + centre_weight * padded[:, :, 1:-1] + side_weight * padded[:, :, 2:]
    second = side_weight * first[:, :, :, :-2] + centre_weight * first[:, :, :, 1:-1] + side_weight * first[:, :, :, 2:]
    return side_weight * second[..., :-2] + centre_weight * second[..., 1:-1] + side_weight * second[..., 2:]

def standardize(smooth):
    windows, frames = (smooth.shape[0], smooth.shape[1])
    series = smooth.reshape(windows, frames, -1)
    centred = series - lax.optimization_barrier(jnp.mean(series, axis=1, keepdims=True))
    spread = lax.optimization_barrier(jnp.mean(centred * centred, axis=1, keepdims=True))
    scored = centred * lax.rsqrt((spread + 1e-05) * frames)
    return jnp.transpose(scored, (2, 0, 1)).astype(jnp.bfloat16)

def reference(bold, gm_index, partners):
    padded = jnp.pad(bold.astype(jnp.float32), ((0, 0), (0, 0), (1, 1), (1, 1), (1, 1)))
    scored = standardize(gaussian_blur(padded))
    row_ids = jnp.arange(NB * BLOCK).astype(jnp.int32)
    slab = row_ids // ROWS_DEV
    slab_row = slab // N_COL
    slab_col = slab % N_COL
    voxel = jnp.maximum(gm_index, 0).astype(jnp.int32)
    local_x = voxel // (SY * SZ)
    local_y = voxel // SZ % SY
    local_z = voxel % SZ
    global_ids = ((slab_row * SX + local_x) * NY + slab_col * SY + local_y) * NZ + local_z
    picked = jnp.take(scored, global_ids.astype(jnp.int32), axis=0)
    panel = jnp.where((gm_index >= 0)[:, None, None], picked, jnp.zeros_like(picked))
    blocks = panel.reshape(NB, BLOCK, W, F)

    def block_tiles(inputs):
        local_block, partner_ids = inputs
        partner_rows = jnp.take(blocks, jnp.maximum(partner_ids, 0).astype(jnp.int32), axis=0)
        tiles_out = jnp.einsum('awf,kbwf->kwab', local_block.astype(jnp.float32), partner_rows.astype(jnp.float32))
        tiles_out = jnp.where((partner_ids >= 0)[:, None, None, None], tiles_out, jnp.zeros_like(tiles_out))
        return tiles_out.astype(jnp.bfloat16)
    return lax.map(block_tiles, (blocks, partners))
```

```python
import functools
import math

import jax
import jax.numpy as jnp
from jax import lax
from jax.experimental import pallas as pl
from jax.experimental.pallas import tpu as pltpu
from jax.sharding import PartitionSpec as P

HOP = 2
MESH = pl.DeviceIdType.MESH

side_weight = math.exp(-0.5) / (1.0 + 2.0 * math.exp(-0.5))
centre_weight = 1.0 / (1.0 + 2.0 * math.exp(-0.5))


def three(low, mid, high):
    return side_weight * low + centre_weight * mid + side_weight * high


def panel_kernel(
    rows,
    gm_ref,
    bold_ref,
    cand_ref,
    halo_lo,
    halo_hi,
    pick,
    xf,
    face_out,
    face_in,
    scored,
    panel,
    halo_send,
    halo_recv,
    face_send,
    face_recv,
    own_sem,
    panel_send,
    panel_recv,
):
    windows, frames, sx, sy, sz = bold_ref.shape
    voxels = sx * sy * sz
    count = gm_ref.shape[1]
    blocks = panel.shape[1]
    r = lax.axis_index("row")
    c = lax.axis_index("col")
    odd = lax.rem(r, 2)
    pair = r + 1 - 2 * odd
    up1 = lax.rem(r + 1, rows)
    down1 = lax.rem(r + rows - 1, rows)
    up2 = lax.rem(r + 2, rows)
    down2 = lax.rem(r + rows - 2, rows)
    other = {"col": 1 - c}

    barrier = pltpu.get_barrier_semaphore()
    pl.semaphore_signal(barrier, inc=1, device_id=other, device_id_type=MESH)
    for target in (up1, down1, up2, down2):
        pl.semaphore_signal(barrier, inc=1, device_id={"row": target}, device_id_type=MESH)
    pl.semaphore_wait(barrier, 5)

    def halo_up(w):
        return pltpu.make_async_remote_copy(
            src_ref=bold_ref.at[w, :, sx - 1],
            dst_ref=halo_lo.at[w],
            send_sem=halo_send.at[w, 0],
            recv_sem=halo_recv.at[w, 0],
            device_id={"row": up1},
            device_id_type=MESH,
        )

    def halo_down(w):
        return pltpu.make_async_remote_copy(
            src_ref=bold_ref.at[w, :, 0],
            dst_ref=halo_hi.at[w],
            send_sem=halo_send.at[w, 1],
            recv_sem=halo_recv.at[w, 1],
            device_id={"row": down1},
            device_id_type=MESH,
        )

    for w in range(windows):

        @pl.when(r < rows - 1)
        def _():
            halo_up(w).start()

        @pl.when(r > 0)
        def _():
            halo_down(w).start()

    @pl.when(r == 0)
    def _():
        halo_lo[...] = jnp.zeros_like(halo_lo)

    @pl.when(r == rows - 1)
    def _():
        halo_hi[...] = jnp.zeros_like(halo_hi)

    gm = gm_ref[...]

    def fill(step, carry):
        start = pl.multiple_of(step * sz, sz)
        ids = lax.broadcasted_iota(jnp.int32, (sz, count), 0) + start
        pick[pl.ds(start, sz), :] = (ids == gm).astype(jnp.float32).astype(jnp.bfloat16)
        return carry

    lax.fori_loop(0, voxels // sz, fill, 0)

    def send(w, src, slot, sem, target):
        return pltpu.make_async_remote_copy(
            src_ref=src,
            dst_ref=cand_ref.at[slot, w],
            send_sem=panel_send.at[w, sem],
            recv_sem=panel_recv.at[w, slot],
            device_id=target,
            device_id_type=MESH,
        )

    def own(w):
        return pltpu.make_async_copy(panel.at[w], cand_ref.at[2 * HOP + c, w], own_sem.at[w])

    def to_other(w):
        return send(w, panel.at[w], 2 * HOP + c, 0, other)

    def to_up2(w):
        return send(w, panel.at[w], c, 1, {"row": up2})

    def to_down2(w):
        return send(w, panel.at[w], 8 + c, 2, {"row": down2})

    def to_pair(w):
        return send(w, panel.at[w], 2 * (1 + 2 * odd) + c, 3, {"row": pair})

    def relay(w):
        mine = 2 * (4 - 4 * odd) + c
        return send(w, cand_ref.at[mine, w], 2 * (3 - 2 * odd) + c, 4, {"row": pair})

    def across(w, which, slot):
        return send(w, cand_ref.at[slot, w], slot, 5 + which, other)

    def arrived(w, slot):
        pltpu.make_async_remote_copy(
            src_ref=cand_ref.at[slot, w],
            dst_ref=cand_ref.at[slot, w],
            send_sem=panel_send.at[w, 0],
            recv_sem=panel_recv.at[w, slot],
            device_id=other,
            device_id_type=MESH,
        ).wait_recv()

    lane = lax.broadcasted_iota(jnp.int32, (1, sz), 1)
    first_lane = lane == 0
    last_lane = lane == sz - 1

    for w in range(windows):

        @pl.when(r > 0)
        def _():
            halo_up(w).wait_recv()

        @pl.when(r < rows - 1)
        def _():
            halo_down(w).wait_recv()

        chunk = 32

        def filter_x(step, carry):
            at = step * chunk
            here = pl.ds(at, chunk)
            low = halo_lo[w, here].astype(jnp.float32)
            first = bold_ref[w, here, 0].astype(jnp.float32)
            second = bold_ref[w, here, 1].astype(jnp.float32)
            high = halo_hi[w, here].astype(jnp.float32)
            flat = pl.ds(pl.multiple_of(at * sy, sy), chunk * sy)
            xf[0, flat, :] = three(low, first, second).reshape(chunk * sy, sz)
            xf[1, flat, :] = three(first, second, high).reshape(chunk * sy, sz)
            return carry

        lax.fori_loop(0, frames // chunk, filter_x, 0)

        for x in range(sx):

            @pl.when(c == 0)
            def _():
                face_out[w, x] = xf[x, pl.ds(sy - 1, frames, stride=sy), :]

            @pl.when(c == 1)
            def _():
                face_out[w, x] = xf[x, pl.ds(0, frames, stride=sy), :]

        face = pltpu.make_async_remote_copy(
            src_ref=face_out.at[w],
            dst_ref=face_in.at[w],
            send_sem=face_send.at[w],
            recv_sem=face_recv.at[w],
            device_id=other,
            device_id_type=MESH,
        )
        face.start()

        def row_of(x, y):
            return xf[x, pl.ds(y, frames, stride=sy), :]

        def finish(x, y, low, mid, high):
            plane = three(low, mid, high)
            left = jnp.where(first_lane, 0.0, pltpu.roll(plane, 1, 1))
            right = jnp.where(last_lane, 0.0, pltpu.roll(plane, sz - 1, 1))
            smooth = three(left, plane, right)
            centred = smooth - jnp.mean(smooth, axis=0, keepdims=True)
            spread = jnp.mean(centred * centred, axis=0, keepdims=True)
            value = centred * lax.rsqrt((spread + 1e-05) * frames)
            at = (x * sy + y) * sz
            scored[:, at : at + sz] = value.astype(jnp.bfloat16)

        for x in range(sx):
            for y in range(1, sy - 1):
                finish(x, y, row_of(x, y - 1), row_of(x, y), row_of(x, y + 1))
        face.wait()
        for x in range(sx):
            edge = face_in[w, x]
            nothing = jnp.zeros_like(edge)
            finish(x, 0, jnp.where(c == 1, edge, nothing), row_of(x, 0), row_of(x, 1))
            finish(x, sy - 1, row_of(x, sy - 2), row_of(x, sy - 1), jnp.where(c == 0, edge, nothing))

        wide = 2 * sz
        for piece in range(count // wide):
            got = jnp.dot(
                scored[...],
                pick[:, piece * wide : (piece + 1) * wide],
                preferred_element_type=jnp.float32,
            ).astype(jnp.bfloat16)
            panel[w, 2 * piece] = got[:, :sz]
            panel[w, 2 * piece + 1] = got[:, sz:]

        to_up2(w).start()
        to_down2(w).start()
        to_pair(w).start()
        to_other(w).start()
        own(w).start()

    order = (
        2 * (3 - 2 * odd) + c,
        2 * (4 - 4 * odd) + c,
        2 * (4 * odd) + c,
        2 * (1 + 2 * odd) + c,
    )
    for w in range(windows):
        arrived(w, order[0])
        across(w, 0, order[0]).start()
        arrived(w, order[1])
        relay(w).start()
        across(w, 1, order[1]).start()
        arrived(w, order[2])
        across(w, 2, order[2]).start()
    for w in range(windows):
        arrived(w, order[3])
        across(w, 3, order[3]).start()

    for w in range(windows):
        for slot in range(2 * HOP + 1):
            arrived(w, 2 * slot + 1 - c)

    for w in range(windows):

        @pl.when(r < rows - 1)
        def _():
            halo_up(w).wait_send()

        @pl.when(r > 0)
        def _():
            halo_down(w).wait_send()

        own(w).wait()
        to_other(w).wait_send()
        to_up2(w).wait_send()
        to_down2(w).wait_send()
        to_pair(w).wait_send()
        relay(w).wait_send()
        for which in range(4):
            across(w, which, order[which]).wait_send()


def tile_kernel(rows, cols, partners_ref, cand_ref, out_ref):
    i = pl.program_id(0)
    blocks = cand_ref.shape[2]
    block_rows = cand_ref.shape[4]
    windows = cand_ref.shape[1]
    slots = out_ref.shape[1]
    r = lax.axis_index("row")
    c = lax.axis_index("col")
    local = [cand_ref[HOP * cols + c, w, i].T for w in range(windows)]
    for k in range(0, slots, 2):
        found = []
        for q in (k, k + 1):
            name = partners_ref[i, q]
            safe = jnp.maximum(name, 0)
            slab = safe // blocks
            distance = lax.rem(slab // cols - r + HOP + rows, rows)
            place = jnp.where(name >= 0, distance * cols + lax.rem(slab, cols), 0)
            found.append((name >= 0, place, lax.rem(safe, blocks)))
        for w in range(windows):
            right = jnp.concatenate([cand_ref[s, w, b] for _, s, b in found], axis=1)
            tiles = jnp.dot(local[w], right, preferred_element_type=jnp.float32)
            for n, (present, _, _) in enumerate(found):
                tile = tiles[:, n * block_rows : (n + 1) * block_rows]
                out_ref[0, k + n, w] = jnp.where(present, tile, 0.0).astype(out_ref.dtype)


def on_device(rows, cols, bold, gm_index, partners):
    windows, frames, sx, sy, sz = bold.shape
    voxels = sx * sy * sz
    count = gm_index.shape[0]
    blocks, slots = partners.shape
    block_rows = count // blocks
    slabs = (2 * HOP + 1) * cols
    bf16, f32 = jnp.bfloat16, jnp.float32
    cand = pl.pallas_call(
        functools.partial(panel_kernel, rows),
        out_shape=jax.ShapeDtypeStruct((slabs, windows, blocks, frames, block_rows), bf16),
        in_specs=[pl.BlockSpec(memory_space=pltpu.VMEM)] * 2,
        out_specs=pl.BlockSpec(memory_space=pl.ANY),
        scratch_shapes=[
            pltpu.VMEM((windows, frames, sy, sz), bf16),
            pltpu.VMEM((windows, frames, sy, sz), bf16),
            pltpu.VMEM((voxels, count), bf16),
            pltpu.VMEM((sx, frames * sy, sz), f32),
            pltpu.VMEM((windows, sx, frames, sz), f32),
            pltpu.VMEM((windows, sx, frames, sz), f32),
            pltpu.VMEM((frames, voxels), bf16),
            pltpu.VMEM((windows, blocks, frames, block_rows), bf16),
            pltpu.SemaphoreType.DMA((windows, 2)),
            pltpu.SemaphoreType.DMA((windows, 2)),
            pltpu.SemaphoreType.DMA((windows,)),
            pltpu.SemaphoreType.DMA((windows,)),
            pltpu.SemaphoreType.DMA((windows,)),
            pltpu.SemaphoreType.DMA((windows, 9)),
            pltpu.SemaphoreType.DMA((windows, slabs)),
        ],
        compiler_params=pltpu.CompilerParams(
            collective_id=0, has_side_effects=True, vmem_limit_bytes=40 * 1024 * 1024
        ),
        name="panels",
    )(gm_index.reshape(1, count), bold)
    return pl.pallas_call(
        functools.partial(tile_kernel, rows, cols),
        out_shape=jax.ShapeDtypeStruct((blocks, slots, windows, block_rows, block_rows), bf16),
        grid_spec=pltpu.PrefetchScalarGridSpec(
            num_scalar_prefetch=1,
            grid=(blocks,),
            in_specs=[pl.BlockSpec(memory_space=pltpu.VMEM)],
            out_specs=pl.BlockSpec(
                (1, slots, windows, block_rows, block_rows), lambda i, names: (i, 0, 0, 0, 0)
            ),
        ),
        compiler_params=pltpu.CompilerParams(vmem_limit_bytes=40 * 1024 * 1024),
        name="tiles",
    )(partners, cand)


def solution(mesh):
    rows, cols = mesh.shape["row"], mesh.shape["col"]
    in_specs = (P("subj", None, "row", "col", None), P(("row", "col")), P(("row", "col"), None))
    out_specs = P(("row", "col"), None, "subj", None, None)
    return jax.shard_map(
        functools.partial(on_device, rows, cols),
        mesh=mesh,
        in_specs=in_specs,
        out_specs=out_specs,
        check_vma=False,
    )
```

```python
import functools
import math

import jax
import jax.numpy as jnp
from jax import lax
from jax.experimental import pallas as pl
from jax.experimental.pallas import tpu as pltpu
from jax.sharding import PartitionSpec as P

HOP = 2
MESH = pl.DeviceIdType.MESH

side_weight = math.exp(-0.5) / (1.0 + 2.0 * math.exp(-0.5))
centre_weight = 1.0 / (1.0 + 2.0 * math.exp(-0.5))


def three(low, mid, high):
    return side_weight * low + centre_weight * mid + side_weight * high


def panel_kernel(
    rows,
    gm_ref,
    bold_ref,
    cand_ref,
    halo_lo,
    halo_hi,
    pick,
    xf,
    face_out,
    face_in,
    scored,
    panel,
    halo_send,
    halo_recv,
    face_send,
    face_recv,
    own_sem,
    panel_send,
    panel_recv,
):
    windows, frames, sx, sy, sz = bold_ref.shape
    voxels = sx * sy * sz
    count = gm_ref.shape[1]
    blocks = panel.shape[1]
    r = lax.axis_index("row")
    c = lax.axis_index("col")
    odd = lax.rem(r, 2)
    pair = r + 1 - 2 * odd
    up1 = lax.rem(r + 1, rows)
    down1 = lax.rem(r + rows - 1, rows)
    up2 = lax.rem(r + 2, rows)
    down2 = lax.rem(r + rows - 2, rows)
    other = {"col": 1 - c}

    barrier = pltpu.get_barrier_semaphore()
    pl.semaphore_signal(barrier, inc=1, device_id=other, device_id_type=MESH)
    for target in (up1, down1, up2, down2):
        pl.semaphore_signal(barrier, inc=1, device_id={"row": target}, device_id_type=MESH)
    pl.semaphore_wait(barrier, 5)

    def halo_up(w):
        return pltpu.make_async_remote_copy(
            src_ref=bold_ref.at[w, :, sx - 1],
            dst_ref=halo_lo.at[w],
            send_sem=halo_send.at[w, 0],
            recv_sem=halo_recv.at[w, 0],
            device_id={"row": up1},
            device_id_type=MESH,
        )

    def halo_down(w):
        return pltpu.make_async_remote_copy(
            src_ref=bold_ref.at[w, :, 0],
            dst_ref=halo_hi.at[w],
            send_sem=halo_send.at[w, 1],
            recv_sem=halo_recv.at[w, 1],
            device_id={"row": down1},
            device_id_type=MESH,
        )

    for w in range(windows):

        @pl.when(r < rows - 1)
        def _():
            halo_up(w).start()

        @pl.when(r > 0)
        def _():
            halo_down(w).start()

    @pl.when(r == 0)
    def _():
        halo_lo[...] = jnp.zeros_like(halo_lo)

    @pl.when(r == rows - 1)
    def _():
        halo_hi[...] = jnp.zeros_like(halo_hi)

    gm = gm_ref[...]

    def fill(step, carry):
        start = pl.multiple_of(step * sz, sz)
        ids = lax.broadcasted_iota(jnp.int32, (sz, count), 0) + start
        pick[pl.ds(start, sz), :] = (ids == gm).astype(jnp.float32).astype(jnp.bfloat16)
        return carry

    lax.fori_loop(0, voxels // sz, fill, 0)

    def send(w, src, slot, sem, target):
        return pltpu.make_async_remote_copy(
            src_ref=src,
            dst_ref=cand_ref.at[slot, w],
            send_sem=panel_send.at[w, sem],
            recv_sem=panel_recv.at[w, slot],
            device_id=target,
            device_id_type=MESH,
        )

    def own(w):
        return pltpu.make_async_copy(panel.at[w], cand_ref.at[2 * HOP + c, w], own_sem.at[w])

    def to_other(w):
        return send(w, panel.at[w], 2 * HOP + c, 0, other)

    def to_up2(w):
        return send(w, panel.at[w], c, 1, {"row": up2})

    def to_down2(w):
        return send(w, panel.at[w], 8 + c, 2, {"row": down2})

    def to_pair(w):
        return send(w, panel.at[w], 2 * (1 + 2 * odd) + c, 3, {"row": pair})

    def relay(w):
        mine = 2 * (4 - 4 * odd) + c
        return send(w, cand_ref.at[mine, w], 2 * (3 - 2 * odd) + c, 4, {"row": pair})

    def across(w, which, slot):
        return send(w, cand_ref.at[slot, w], slot, 5 + which, other)

    def arrived(w, slot):
        pltpu.make_async_remote_copy(
            src_ref=cand_ref.at[slot, w],
            dst_ref=cand_ref.at[slot, w],
            send_sem=panel_send.at[w, 0],
            recv_sem=panel_recv.at[w, slot],
            device_id=other,
            device_id_type=MESH,
        ).wait_recv()

    lane = lax.broadcasted_iota(jnp.int32, (1, sz), 1)
    first_lane = lane == 0
    last_lane = lane == sz - 1

    for w in range(windows):

        @pl.when(r > 0)
        def _():
            halo_up(w).wait_recv()

        @pl.when(r < rows - 1)
        def _():
            halo_down(w).wait_recv()

        if w > 0:
            to_pair(w - 1).start()
        chunk = 32

        def filter_x(step, carry):
            at = step * chunk
            here = pl.ds(at, chunk)
            low = halo_lo[w, here].astype(jnp.float32)
            first = bold_ref[w, here, 0].astype(jnp.float32)
            second = bold_ref[w, here, 1].astype(jnp.float32)
            high = halo_hi[w, here].astype(jnp.float32)
            flat = pl.ds(pl.multiple_of(at * sy, sy), chunk * sy)
            xf[0, flat, :] = three(low, first, second).reshape(chunk * sy, sz)
            xf[1, flat, :] = three(first, second, high).reshape(chunk * sy, sz)
            return carry

        lax.fori_loop(0, frames // chunk, filter_x, 0)

        for x in range(sx):

            @pl.when(c == 0)
            def _():
                face_out[w, x] = xf[x, pl.ds(sy - 1, frames, stride=sy), :]

            @pl.when(c == 1)
            def _():
                face_out[w, x] = xf[x, pl.ds(0, frames, stride=sy), :]

        face = pltpu.make_async_remote_copy(
            src_ref=face_out.at[w],
            dst_ref=face_in.at[w],
            send_sem=face_send.at[w],
            recv_sem=face_recv.at[w],
            device_id=other,
            device_id_type=MESH,
        )
        face.start()

        def row_of(x, y):
            return xf[x, pl.ds(y, frames, stride=sy), :]

        def finish(x, y, low, mid, high):
            plane = three(low, mid, high)
            left = jnp.where(first_lane, 0.0, pltpu.roll(plane, 1, 1))
            right = jnp.where(last_lane, 0.0, pltpu.roll(plane, sz - 1, 1))
            smooth = three(left, plane, right)
            centred = smooth - jnp.mean(smooth, axis=0, keepdims=True)
            spread = jnp.mean(centred * centred, axis=0, keepdims=True)
            value = centred * lax.rsqrt((spread + 1e-05) * frames)
            at = (x * sy + y) * sz
            scored[:, at : at + sz] = value.astype(jnp.bfloat16)

        for x in range(sx):
            for y in range(1, sy - 1):
                finish(x, y, row_of(x, y - 1), row_of(x, y), row_of(x, y + 1))
        face.wait()
        for x in range(sx):
            edge = face_in[w, x]
            nothing = jnp.zeros_like(edge)
            finish(x, 0, jnp.where(c == 1, edge, nothing), row_of(x, 0), row_of(x, 1))
            finish(x, sy - 1, row_of(x, sy - 2), row_of(x, sy - 1), jnp.where(c == 0, edge, nothing))

        wide = 2 * sz
        for piece in range(count // wide):
            got = jnp.dot(
                scored[...],
                pick[:, piece * wide : (piece + 1) * wide],
                preferred_element_type=jnp.float32,
            ).astype(jnp.bfloat16)
            panel[w, 2 * piece] = got[:, :sz]
            panel[w, 2 * piece + 1] = got[:, sz:]

        to_up2(w).start()
        to_down2(w).start()
        if w > 0:
            to_pair(w).start()
        to_other(w).start()
        own(w).start()

    order = (
        2 * (3 - 2 * odd) + c,
        2 * (4 - 4 * odd) + c,
        2 * (4 * odd) + c,
        2 * (1 + 2 * odd) + c,
    )
    inside = r + (rows - 2 * r - 1) * odd < rows - 2

    def relay_far(w):
        target = up2 + (down2 - up2) * odd
        return send(w, cand_ref.at[order[0], w], 2 * (1 + 2 * odd) + c, 4, {"row": target})

    def pass_on(w, which):
        arrived(w, order[which])
        across(w, which, order[which]).start()

    pass_on(0, 1)
    relay(0).start()
    pass_on(0, 2)
    pass_on(0, 0)
    pass_on(1, 0)

    @pl.when(inside)
    def _():
        relay_far(1).start()

    pass_on(1, 1)

    @pl.when(jnp.logical_not(inside))
    def _():
        relay(1).start()

    pass_on(1, 2)
    pass_on(0, 3)
    pass_on(1, 3)

    for w in range(windows):
        for slot in range(2 * HOP + 1):
            arrived(w, 2 * slot + 1 - c)

    for w in range(windows):

        @pl.when(r < rows - 1)
        def _():
            halo_up(w).wait_send()

        @pl.when(r > 0)
        def _():
            halo_down(w).wait_send()

        own(w).wait()
        to_other(w).wait_send()
        to_up2(w).wait_send()
        to_down2(w).wait_send()
        to_pair(w).wait_send()
        if w == 0:
            relay(w).wait_send()
        else:

            @pl.when(inside)
            def _():
                relay_far(w).wait_send()

            @pl.when(jnp.logical_not(inside))
            def _():
                relay(w).wait_send()

        for which in range(4):
            across(w, which, order[which]).wait_send()


def tile_kernel(rows, cols, partners_ref, cand_ref, out_ref):
    i = pl.program_id(1)
    blocks = cand_ref.shape[2]
    block_rows = cand_ref.shape[4]
    slots = out_ref.shape[1]
    r = lax.axis_index("row")
    c = lax.axis_index("col")
    local = cand_ref[HOP * cols + c, 0, i].T
    for k in range(0, slots, 2):
        found = []
        for q in (k, k + 1):
            name = partners_ref[i, q]
            safe = jnp.maximum(name, 0)
            slab = safe // blocks
            distance = lax.rem(slab // cols - r + HOP + rows, rows)
            place = jnp.where(name >= 0, distance * cols + lax.rem(slab, cols), 0)
            found.append((name >= 0, place, lax.rem(safe, blocks)))
        right = jnp.concatenate([cand_ref[s, 0, b] for _, s, b in found], axis=1)
        tiles = jnp.dot(local, right, preferred_element_type=jnp.float32)
        for n, (present, _, _) in enumerate(found):
            tile = tiles[:, n * block_rows : (n + 1) * block_rows]
            out_ref[0, k + n, 0] = jnp.where(present, tile, 0.0).astype(out_ref.dtype)


def on_device(rows, cols, bold, gm_index, partners):
    windows, frames, sx, sy, sz = bold.shape
    voxels = sx * sy * sz
    count = gm_index.shape[0]
    blocks, slots = partners.shape
    block_rows = count // blocks
    slabs = (2 * HOP + 1) * cols
    bf16, f32 = jnp.bfloat16, jnp.float32
    cand = pl.pallas_call(
        functools.partial(panel_kernel, rows),
        out_shape=jax.ShapeDtypeStruct((slabs, windows, blocks, frames, block_rows), bf16),
        in_specs=[pl.BlockSpec(memory_space=pltpu.VMEM)] * 2,
        out_specs=pl.BlockSpec(memory_space=pl.ANY),
        scratch_shapes=[
            pltpu.VMEM((windows, frames, sy, sz), bf16),
            pltpu.VMEM((windows, frames, sy, sz), bf16),
            pltpu.VMEM((voxels, count), bf16),
            pltpu.VMEM((sx, frames * sy, sz), f32),
            pltpu.VMEM((windows, sx, frames, sz), f32),
            pltpu.VMEM((windows, sx, frames, sz), f32),
            pltpu.VMEM((frames, voxels), bf16),
            pltpu.VMEM((windows, blocks, frames, block_rows), bf16),
            pltpu.SemaphoreType.DMA((windows, 2)),
            pltpu.SemaphoreType.DMA((windows, 2)),
            pltpu.SemaphoreType.DMA((windows,)),
            pltpu.SemaphoreType.DMA((windows,)),
            pltpu.SemaphoreType.DMA((windows,)),
            pltpu.SemaphoreType.DMA((windows, 9)),
            pltpu.SemaphoreType.DMA((windows, slabs)),
        ],
        compiler_params=pltpu.CompilerParams(
            collective_id=0, has_side_effects=True, vmem_limit_bytes=40 * 1024 * 1024
        ),
        name="panels",
    )(gm_index.reshape(1, count), bold)
    return pl.pallas_call(
        functools.partial(tile_kernel, rows, cols),
        out_shape=jax.ShapeDtypeStruct((blocks, slots, windows, block_rows, block_rows), bf16),
        grid_spec=pltpu.PrefetchScalarGridSpec(
            num_scalar_prefetch=1,
            grid=(windows, blocks),
            in_specs=[
                pl.BlockSpec(
                    (slabs, 1, blocks, frames, block_rows), lambda w, i, names: (0, w, 0, 0, 0)
                )
            ],
            out_specs=pl.BlockSpec(
                (1, slots, 1, block_rows, block_rows), lambda w, i, names: (i, 0, w, 0, 0)
            ),
        ),
        compiler_params=pltpu.CompilerParams(vmem_limit_bytes=40 * 1024 * 1024),
        name="tiles",
    )(partners, cand)


def solution(mesh):
    rows, cols = mesh.shape["row"], mesh.shape["col"]
    in_specs = (P("subj", None, "row", "col", None), P(("row", "col")), P(("row", "col"), None))
    out_specs = P(("row", "col"), None, "subj", None, None)
    return jax.shard_map(
        functools.partial(on_device, rows, cols),
        mesh=mesh,
        in_specs=in_specs,
        out_specs=out_specs,
        check_vma=False,
    )
```

```python
import functools
import math

import jax
import jax.numpy as jnp
from jax import lax
from jax.experimental import pallas as pl
from jax.experimental.pallas import tpu as pltpu
from jax.sharding import PartitionSpec as P

HOP = 2
MESH = pl.DeviceIdType.MESH

side_weight = math.exp(-0.5) / (1.0 + 2.0 * math.exp(-0.5))
centre_weight = 1.0 / (1.0 + 2.0 * math.exp(-0.5))


def three(low, mid, high):
    return side_weight * low + centre_weight * mid + side_weight * high


def panel_kernel(
    rows,
    gm_ref,
    bold_ref,
    cand_ref,
    halo,
    halo_via,
    pick,
    xf,
    face_out,
    face_in,
    scored,
    panel,
    halo_send,
    halo_recv,
    face_send,
    face_recv,
    own_sem,
    panel_send,
    panel_recv,
):
    windows, frames, sx, sy, sz = bold_ref.shape
    voxels = sx * sy * sz
    count = gm_ref.shape[1]
    blocks = panel.shape[1]
    r = lax.axis_index("row")
    c = lax.axis_index("col")
    odd = lax.rem(r, 2)
    pair = r + 1 - 2 * odd
    up1 = lax.rem(r + 1, rows)
    down1 = lax.rem(r + rows - 1, rows)
    up2 = lax.rem(r + 2, rows)
    down2 = lax.rem(r + rows - 2, rows)
    other = {"col": 1 - c}

    barrier = pltpu.get_barrier_semaphore()
    pl.semaphore_signal(barrier, inc=1, device_id=other, device_id_type=MESH)
    for target in (up1, down1, up2, down2):
        pl.semaphore_signal(barrier, inc=1, device_id={"row": target}, device_id_type=MESH)
    pl.semaphore_wait(barrier, 5)

    far = up2 * odd + down2 * (1 - odd)
    inside = r + (rows - 2 * r - 1) * odd < rows - 2
    far_side = r + (rows - 2 * r - 1) * odd > 0

    def halo_copy(w, src, dst, sem, target):
        return pltpu.make_async_remote_copy(
            src_ref=src,
            dst_ref=dst,
            send_sem=halo_send.at[w, sem],
            recv_sem=halo_recv.at[w, sem],
            device_id={"row": target},
            device_id_type=MESH,
        )

    def halo_far(w):
        return halo_copy(w, bold_ref.at[w, :, (sx - 1) * odd], halo_via.at[w], 0, far)

    def halo_pair(w):
        return halo_copy(w, bold_ref.at[w, :, (sx - 1) * (1 - odd)], halo.at[odd, w], 1, pair)

    def halo_relay(w):
        return halo_copy(w, halo_via.at[w], halo.at[1 - odd, w], 2, pair)

    for w in range(windows):

        @pl.when(far_side)
        def _():
            halo_far(w).start()

    halo_pair(0).start()

    @pl.when(r == 0)
    def _():
        halo[0] = jnp.zeros_like(halo[0])

    @pl.when(r == rows - 1)
    def _():
        halo[1] = jnp.zeros_like(halo[1])

    gm = gm_ref[...]

    def fill(step, carry):
        start = pl.multiple_of(step * sz, sz)
        ids = lax.broadcasted_iota(jnp.int32, (sz, count), 0) + start
        pick[pl.ds(start, sz), :] = (ids == gm).astype(jnp.float32).astype(jnp.bfloat16)
        return carry

    lax.fori_loop(0, voxels // sz, fill, 0)

    for w in range(windows):

        @pl.when(inside)
        def _():
            halo_far(w).wait_recv()
            halo_relay(w).start()

        if w + 1 < windows:
            halo_pair(w + 1).start()

    def send(w, src, slot, sem, target):
        return pltpu.make_async_remote_copy(
            src_ref=src,
            dst_ref=cand_ref.at[slot, w],
            send_sem=panel_send.at[w, sem],
            recv_sem=panel_recv.at[w, slot],
            device_id=target,
            device_id_type=MESH,
        )

    def own(w):
        return pltpu.make_async_copy(panel.at[w], cand_ref.at[2 * HOP + c, w], own_sem.at[w])

    def to_other(w):
        return send(w, panel.at[w], 2 * HOP + c, 0, other)

    def to_up2(w):
        return send(w, panel.at[w], c, 1, {"row": up2})

    def to_down2(w):
        return send(w, panel.at[w], 8 + c, 2, {"row": down2})

    def to_pair(w):
        return send(w, panel.at[w], 2 * (1 + 2 * odd) + c, 3, {"row": pair})

    def relay(w):
        mine = 2 * (4 - 4 * odd) + c
        return send(w, cand_ref.at[mine, w], 2 * (3 - 2 * odd) + c, 4, {"row": pair})

    def across(w, which, slot):
        return send(w, cand_ref.at[slot, w], slot, 5 + which, other)

    def arrived(w, slot):
        pltpu.make_async_remote_copy(
            src_ref=cand_ref.at[slot, w],
            dst_ref=cand_ref.at[slot, w],
            send_sem=panel_send.at[w, 0],
            recv_sem=panel_recv.at[w, slot],
            device_id=other,
            device_id_type=MESH,
        ).wait_recv()

    lane = lax.broadcasted_iota(jnp.int32, (1, sz), 1)
    first_lane = lane == 0
    last_lane = lane == sz - 1

    for w in range(windows):

        halo_pair(w).wait_recv()

        @pl.when(far_side)
        def _():
            halo_relay(w).wait_recv()

        if w > 0:
            to_pair(w - 1).start()
        chunk = 32

        def filter_x(step, carry):
            at = step * chunk
            here = pl.ds(at, chunk)
            low = halo[0, w, here].astype(jnp.float32)
            first = bold_ref[w, here, 0].astype(jnp.float32)
            second = bold_ref[w, here, 1].astype(jnp.float32)
            high = halo[1, w, here].astype(jnp.float32)
            flat = pl.ds(pl.multiple_of(at * sy, sy), chunk * sy)
            xf[0, flat, :] = three(low, first, second).reshape(chunk * sy, sz)
            xf[1, flat, :] = three(first, second, high).reshape(chunk * sy, sz)
            return carry

        lax.fori_loop(0, frames // chunk, filter_x, 0)

        for x in range(sx):

            @pl.when(c == 0)
            def _():
                face_out[w, x] = xf[x, pl.ds(sy - 1, frames, stride=sy), :]

            @pl.when(c == 1)
            def _():
                face_out[w, x] = xf[x, pl.ds(0, frames, stride=sy), :]

        face = pltpu.make_async_remote_copy(
            src_ref=face_out.at[w],
            dst_ref=face_in.at[w],
            send_sem=face_send.at[w],
            recv_sem=face_recv.at[w],
            device_id=other,
            device_id_type=MESH,
        )
        face.start()

        def row_of(x, y):
            return xf[x, pl.ds(y, frames, stride=sy), :]

        def finish(x, y, low, mid, high):
            plane = three(low, mid, high)
            left = jnp.where(first_lane, 0.0, pltpu.roll(plane, 1, 1))
            right = jnp.where(last_lane, 0.0, pltpu.roll(plane, sz - 1, 1))
            smooth = three(left, plane, right)
            centred = smooth - jnp.mean(smooth, axis=0, keepdims=True)
            spread = jnp.mean(centred * centred, axis=0, keepdims=True)
            value = centred * lax.rsqrt((spread + 1e-05) * frames)
            at = (x * sy + y) * sz
            scored[:, at : at + sz] = value.astype(jnp.bfloat16)

        for x in range(sx):
            for y in range(1, sy - 1):
                finish(x, y, row_of(x, y - 1), row_of(x, y), row_of(x, y + 1))
        face.wait()
        for x in range(sx):
            edge = face_in[w, x]
            nothing = jnp.zeros_like(edge)
            finish(x, 0, jnp.where(c == 1, edge, nothing), row_of(x, 0), row_of(x, 1))
            finish(x, sy - 1, row_of(x, sy - 2), row_of(x, sy - 1), jnp.where(c == 0, edge, nothing))

        wide = 2 * sz
        for piece in range(count // wide):
            got = jnp.dot(
                scored[...],
                pick[:, piece * wide : (piece + 1) * wide],
                preferred_element_type=jnp.float32,
            ).astype(jnp.bfloat16)
            panel[w, 2 * piece] = got[:, :sz]
            panel[w, 2 * piece + 1] = got[:, sz:]

        to_up2(w).start()
        to_down2(w).start()
        if w > 0:
            to_pair(w).start()
        to_other(w).start()
        own(w).start()

    order = (
        2 * (3 - 2 * odd) + c,
        2 * (4 - 4 * odd) + c,
        2 * (4 * odd) + c,
        2 * (1 + 2 * odd) + c,
    )

    def relay_far(w):
        target = up2 + (down2 - up2) * odd
        return send(w, cand_ref.at[order[0], w], 2 * (1 + 2 * odd) + c, 4, {"row": target})

    def pass_on(w, which):
        arrived(w, order[which])
        across(w, which, order[which]).start()

    pass_on(0, 1)
    relay(0).start()
    pass_on(0, 2)
    pass_on(0, 0)
    pass_on(1, 0)

    @pl.when(inside)
    def _():
        relay_far(1).start()

    pass_on(1, 1)

    @pl.when(jnp.logical_not(inside))
    def _():
        relay(1).start()

    pass_on(1, 2)
    pass_on(0, 3)
    pass_on(1, 3)

    for w in range(windows):
        for slot in range(2 * HOP + 1):
            arrived(w, 2 * slot + 1 - c)

    for w in range(windows):

        halo_pair(w).wait_send()

        @pl.when(far_side)
        def _():
            halo_far(w).wait_send()

        @pl.when(inside)
        def _():
            halo_relay(w).wait_send()

        own(w).wait()
        to_other(w).wait_send()
        to_up2(w).wait_send()
        to_down2(w).wait_send()
        to_pair(w).wait_send()
        if w == 0:
            relay(w).wait_send()
        else:

            @pl.when(inside)
            def _():
                relay_far(w).wait_send()

            @pl.when(jnp.logical_not(inside))
            def _():
                relay(w).wait_send()

        for which in range(4):
            across(w, which, order[which]).wait_send()


def tile_kernel(rows, cols, partners_ref, cand_ref, out_ref):
    i = pl.program_id(0)
    blocks = cand_ref.shape[2]
    block_rows = cand_ref.shape[4]
    windows = cand_ref.shape[1]
    slots = out_ref.shape[1]
    r = lax.axis_index("row")
    c = lax.axis_index("col")
    local = [cand_ref[HOP * cols + c, w, i].T for w in range(windows)]
    for k in range(0, slots, 2):
        found = []
        for q in (k, k + 1):
            name = partners_ref[i, q]
            safe = jnp.maximum(name, 0)
            slab = safe // blocks
            distance = lax.rem(slab // cols - r + HOP + rows, rows)
            place = jnp.where(name >= 0, distance * cols + lax.rem(slab, cols), 0)
            found.append((name >= 0, place, lax.rem(safe, blocks)))
        for w in range(windows):
            right = jnp.concatenate([cand_ref[s, w, b] for _, s, b in found], axis=1)
            tiles = jnp.dot(local[w], right, preferred_element_type=jnp.float32)
            for n, (present, _, _) in enumerate(found):
                tile = tiles[:, n * block_rows : (n + 1) * block_rows]
                out_ref[0, k + n, w] = jnp.where(present, tile, 0.0).astype(out_ref.dtype)


def on_device(rows, cols, bold, gm_index, partners):
    windows, frames, sx, sy, sz = bold.shape
    voxels = sx * sy * sz
    count = gm_index.shape[0]
    blocks, slots = partners.shape
    block_rows = count // blocks
    slabs = (2 * HOP + 1) * cols
    bf16, f32 = jnp.bfloat16, jnp.float32
    cand = pl.pallas_call(
        functools.partial(panel_kernel, rows),
        out_shape=jax.ShapeDtypeStruct((slabs, windows, blocks, frames, block_rows), bf16),
        in_specs=[pl.BlockSpec(memory_space=pltpu.VMEM)] * 2,
        out_specs=pl.BlockSpec(memory_space=pl.ANY),
        scratch_shapes=[
            pltpu.VMEM((2, windows, frames, sy, sz), bf16),
            pltpu.VMEM((windows, frames, sy, sz), bf16),
            pltpu.VMEM((voxels, count), bf16),
            pltpu.VMEM((sx, frames * sy, sz), f32),
            pltpu.VMEM((windows, sx, frames, sz), f32),
            pltpu.VMEM((windows, sx, frames, sz), f32),
            pltpu.VMEM((frames, voxels), bf16),
            pltpu.VMEM((windows, blocks, frames, block_rows), bf16),
            pltpu.SemaphoreType.DMA((windows, 3)),
            pltpu.SemaphoreType.DMA((windows, 3)),
            pltpu.SemaphoreType.DMA((windows,)),
            pltpu.SemaphoreType.DMA((windows,)),
            pltpu.SemaphoreType.DMA((windows,)),
            pltpu.SemaphoreType.DMA((windows, 9)),
            pltpu.SemaphoreType.DMA((windows, slabs)),
        ],
        compiler_params=pltpu.CompilerParams(
            collective_id=0, has_side_effects=True, vmem_limit_bytes=40 * 1024 * 1024
        ),
        name="panels",
    )(gm_index.reshape(1, count), bold)
    return pl.pallas_call(
        functools.partial(tile_kernel, rows, cols),
        out_shape=jax.ShapeDtypeStruct((blocks, slots, windows, block_rows, block_rows), bf16),
        grid_spec=pltpu.PrefetchScalarGridSpec(
            num_scalar_prefetch=1,
            grid=(blocks,),
            in_specs=[pl.BlockSpec(memory_space=pltpu.VMEM)],
            out_specs=pl.BlockSpec(
                (1, slots, windows, block_rows, block_rows), lambda i, names: (i, 0, 0, 0, 0)
            ),
        ),
        compiler_params=pltpu.CompilerParams(vmem_limit_bytes=40 * 1024 * 1024),
        name="tiles",
    )(partners, cand)


def solution(mesh):
    rows, cols = mesh.shape["row"], mesh.shape["col"]
    in_specs = (P("subj", None, "row", "col", None), P(("row", "col")), P(("row", "col"), None))
    out_specs = P(("row", "col"), None, "subj", None, None)
    return jax.shard_map(
        functools.partial(on_device, rows, cols),
        mesh=mesh,
        in_specs=in_specs,
        out_specs=out_specs,
        check_vma=False,
    )
```

```python
import functools
import math

import jax
import jax.numpy as jnp
from jax import lax
from jax.experimental import pallas as pl
from jax.experimental.pallas import tpu as pltpu
from jax.sharding import PartitionSpec as P

HOP = 2
MESH = pl.DeviceIdType.MESH

side_weight = math.exp(-0.5) / (1.0 + 2.0 * math.exp(-0.5))
centre_weight = 1.0 / (1.0 + 2.0 * math.exp(-0.5))


def three(low, mid, high):
    return side_weight * low + centre_weight * mid + side_weight * high


def panel_kernel(
    rows,
    gm_ref,
    bold_ref,
    cand_ref,
    held,
    halo,
    halo_via,
    pick,
    xf,
    face_out,
    face_in,
    scored,
    panel,
    load_sem,
    halo_send,
    halo_recv,
    face_send,
    face_recv,
    own_sem,
    panel_send,
    panel_recv,
):
    windows, frames, sx, sy, sz = bold_ref.shape
    voxels = sx * sy * sz
    count = gm_ref.shape[1]
    blocks = panel.shape[1]
    r = lax.axis_index("row")
    c = lax.axis_index("col")
    odd = lax.rem(r, 2)
    pair = r + 1 - 2 * odd
    up1 = lax.rem(r + 1, rows)
    down1 = lax.rem(r + rows - 1, rows)
    up2 = lax.rem(r + 2, rows)
    down2 = lax.rem(r + rows - 2, rows)
    other = {"col": 1 - c}

    load = pltpu.make_async_copy(bold_ref, held, load_sem)
    load.start()
    barrier = pltpu.get_barrier_semaphore()
    pl.semaphore_signal(barrier, inc=1, device_id=other, device_id_type=MESH)
    for target in (up1, down1, up2, down2):
        pl.semaphore_signal(barrier, inc=1, device_id={"row": target}, device_id_type=MESH)
    pl.semaphore_wait(barrier, 5)

    far = up2 * odd + down2 * (1 - odd)
    inside = r + (rows - 2 * r - 1) * odd < rows - 2
    far_side = r + (rows - 2 * r - 1) * odd > 0

    def halo_copy(w, src, dst, sem, target):
        return pltpu.make_async_remote_copy(
            src_ref=src,
            dst_ref=dst,
            send_sem=halo_send.at[w, sem],
            recv_sem=halo_recv.at[w, sem],
            device_id={"row": target},
            device_id_type=MESH,
        )

    def halo_far(w):
        return halo_copy(w, bold_ref.at[w, :, (sx - 1) * odd], halo_via.at[w], 0, far)

    def halo_pair(w):
        return halo_copy(w, bold_ref.at[w, :, (sx - 1) * (1 - odd)], halo.at[odd, w], 1, pair)

    def halo_relay(w):
        return halo_copy(w, halo_via.at[w], halo.at[1 - odd, w], 2, pair)

    for w in range(windows):

        @pl.when(far_side)
        def _():
            halo_far(w).start()

    halo_pair(0).start()

    @pl.when(r == 0)
    def _():
        halo[0] = jnp.zeros_like(halo[0])

    @pl.when(r == rows - 1)
    def _():
        halo[1] = jnp.zeros_like(halo[1])

    gm = gm_ref[...]

    def fill(step, carry):
        start = pl.multiple_of(step * sz, sz)
        ids = lax.broadcasted_iota(jnp.int32, (sz, count), 0) + start
        pick[pl.ds(start, sz), :] = (ids == gm).astype(jnp.float32).astype(jnp.bfloat16)
        return carry

    lax.fori_loop(0, voxels // sz, fill, 0)

    def pass_halo(w):
        @pl.when(inside)
        def _():
            halo_far(w).wait_recv()
            halo_relay(w).start()

    pass_halo(0)
    for w in range(1, windows):
        halo_pair(w).start()
    load.wait()

    def send(w, src, slot, sem, target):
        return pltpu.make_async_remote_copy(
            src_ref=src,
            dst_ref=cand_ref.at[slot, w],
            send_sem=panel_send.at[w, sem],
            recv_sem=panel_recv.at[w, slot],
            device_id=target,
            device_id_type=MESH,
        )

    def own(w):
        return pltpu.make_async_copy(panel.at[w], cand_ref.at[2 * HOP + c, w], own_sem.at[w])

    def to_other(w):
        return send(w, panel.at[w], 2 * HOP + c, 0, other)

    def to_up2(w):
        return send(w, panel.at[w], c, 1, {"row": up2})

    def to_down2(w):
        return send(w, panel.at[w], 8 + c, 2, {"row": down2})

    def to_pair(w):
        return send(w, panel.at[w], 2 * (1 + 2 * odd) + c, 3, {"row": pair})

    def relay(w):
        mine = 2 * (4 - 4 * odd) + c
        return send(w, cand_ref.at[mine, w], 2 * (3 - 2 * odd) + c, 4, {"row": pair})

    def across(w, which, slot):
        return send(w, cand_ref.at[slot, w], slot, 5 + which, other)

    def arrived(w, slot):
        pltpu.make_async_remote_copy(
            src_ref=cand_ref.at[slot, w],
            dst_ref=cand_ref.at[slot, w],
            send_sem=panel_send.at[w, 0],
            recv_sem=panel_recv.at[w, slot],
            device_id=other,
            device_id_type=MESH,
        ).wait_recv()

    lane = lax.broadcasted_iota(jnp.int32, (1, sz), 1)
    first_lane = lane == 0
    last_lane = lane == sz - 1

    for w in range(windows):

        if w > 0:
            pass_halo(w)
        halo_pair(w).wait_recv()

        @pl.when(far_side)
        def _():
            halo_relay(w).wait_recv()

        if w > 0:
            to_pair(w - 1).start()
        chunk = 32

        def filter_x(step, carry):
            at = step * chunk
            here = pl.ds(at, chunk)
            low = halo[0, w, here].astype(jnp.float32)
            first = held[w, here, 0].astype(jnp.float32)
            second = held[w, here, 1].astype(jnp.float32)
            high = halo[1, w, here].astype(jnp.float32)
            flat = pl.ds(pl.multiple_of(at * sy, sy), chunk * sy)
            xf[0, flat, :] = three(low, first, second).reshape(chunk * sy, sz)
            xf[1, flat, :] = three(first, second, high).reshape(chunk * sy, sz)
            return carry

        lax.fori_loop(0, frames // chunk, filter_x, 0)

        for x in range(sx):

            @pl.when(c == 0)
            def _():
                face_out[w, x] = xf[x, pl.ds(sy - 1, frames, stride=sy), :]

            @pl.when(c == 1)
            def _():
                face_out[w, x] = xf[x, pl.ds(0, frames, stride=sy), :]

        face = pltpu.make_async_remote_copy(
            src_ref=face_out.at[w],
            dst_ref=face_in.at[w],
            send_sem=face_send.at[w],
            recv_sem=face_recv.at[w],
            device_id=other,
            device_id_type=MESH,
        )
        face.start()

        def row_of(x, y):
            return xf[x, pl.ds(y, frames, stride=sy), :]

        def finish(x, y, low, mid, high):
            plane = three(low, mid, high)
            left = jnp.where(first_lane, 0.0, pltpu.roll(plane, 1, 1))
            right = jnp.where(last_lane, 0.0, pltpu.roll(plane, sz - 1, 1))
            smooth = three(left, plane, right)
            centred = smooth - jnp.mean(smooth, axis=0, keepdims=True)
            spread = jnp.mean(centred * centred, axis=0, keepdims=True)
            value = centred * lax.rsqrt((spread + 1e-05) * frames)
            at = (x * sy + y) * sz
            scored[:, at : at + sz] = value.astype(jnp.bfloat16)

        for x in range(sx):
            for y in range(1, sy - 1):
                finish(x, y, row_of(x, y - 1), row_of(x, y), row_of(x, y + 1))
        face.wait()
        for x in range(sx):
            edge = face_in[w, x]
            nothing = jnp.zeros_like(edge)
            finish(x, 0, jnp.where(c == 1, edge, nothing), row_of(x, 0), row_of(x, 1))
            finish(x, sy - 1, row_of(x, sy - 2), row_of(x, sy - 1), jnp.where(c == 0, edge, nothing))

        wide = 2 * sz
        for piece in range(count // wide):
            got = jnp.dot(
                scored[...],
                pick[:, piece * wide : (piece + 1) * wide],
                preferred_element_type=jnp.float32,
            ).astype(jnp.bfloat16)
            panel[w, 2 * piece] = got[:, :sz]
            panel[w, 2 * piece + 1] = got[:, sz:]

        to_up2(w).start()
        to_down2(w).start()
        if w > 0:
            to_pair(w).start()
        to_other(w).start()
        own(w).start()

    order = (
        2 * (3 - 2 * odd) + c,
        2 * (4 - 4 * odd) + c,
        2 * (4 * odd) + c,
        2 * (1 + 2 * odd) + c,
    )

    def relay_far(w):
        target = up2 + (down2 - up2) * odd
        return send(w, cand_ref.at[order[0], w], 2 * (1 + 2 * odd) + c, 4, {"row": target})

    def pass_on(w, which):
        arrived(w, order[which])
        across(w, which, order[which]).start()

    pass_on(0, 1)
    relay(0).start()
    pass_on(0, 2)
    pass_on(0, 0)
    pass_on(1, 0)

    @pl.when(inside)
    def _():
        relay_far(1).start()

    pass_on(1, 1)

    @pl.when(jnp.logical_not(inside))
    def _():
        relay(1).start()

    pass_on(1, 2)
    pass_on(0, 3)
    pass_on(1, 3)

    for w in range(windows):
        for slot in range(2 * HOP + 1):
            arrived(w, 2 * slot + 1 - c)

    for w in range(windows):

        halo_pair(w).wait_send()

        @pl.when(far_side)
        def _():
            halo_far(w).wait_send()

        @pl.when(inside)
        def _():
            halo_relay(w).wait_send()

        own(w).wait()
        to_other(w).wait_send()
        to_up2(w).wait_send()
        to_down2(w).wait_send()
        to_pair(w).wait_send()
        if w == 0:
            relay(w).wait_send()
        else:

            @pl.when(inside)
            def _():
                relay_far(w).wait_send()

            @pl.when(jnp.logical_not(inside))
            def _():
                relay(w).wait_send()

        for which in range(4):
            across(w, which, order[which]).wait_send()


def tile_kernel(rows, cols, partners_ref, cand_ref, out_ref):
    i = pl.program_id(0)
    blocks = cand_ref.shape[2]
    block_rows = cand_ref.shape[4]
    windows = cand_ref.shape[1]
    slots = out_ref.shape[1]
    r = lax.axis_index("row")
    c = lax.axis_index("col")
    local = [cand_ref[HOP * cols + c, w, i].T for w in range(windows)]
    for k in range(0, slots, 2):
        found = []
        for q in (k, k + 1):
            name = partners_ref[i, q]
            safe = jnp.maximum(name, 0)
            slab = safe // blocks
            distance = lax.rem(slab // cols - r + HOP + rows, rows)
            place = jnp.where(name >= 0, distance * cols + lax.rem(slab, cols), 0)
            found.append((name >= 0, place, lax.rem(safe, blocks)))
        for w in range(windows):
            right = jnp.concatenate([cand_ref[s, w, b] for _, s, b in found], axis=1)
            tiles = jnp.dot(local[w], right, preferred_element_type=jnp.float32)
            for n, (present, _, _) in enumerate(found):
                tile = tiles[:, n * block_rows : (n + 1) * block_rows]
                out_ref[0, k + n, w] = jnp.where(present, tile, 0.0).astype(out_ref.dtype)


def on_device(rows, cols, bold, gm_index, partners):
    windows, frames, sx, sy, sz = bold.shape
    voxels = sx * sy * sz
    count = gm_index.shape[0]
    blocks, slots = partners.shape
    block_rows = count // blocks
    slabs = (2 * HOP + 1) * cols
    bf16, f32 = jnp.bfloat16, jnp.float32
    cand = pl.pallas_call(
        functools.partial(panel_kernel, rows),
        out_shape=jax.ShapeDtypeStruct((slabs, windows, blocks, frames, block_rows), bf16),
        in_specs=[
            pl.BlockSpec(memory_space=pltpu.VMEM),
            pl.BlockSpec(memory_space=pl.ANY),
        ],
        out_specs=pl.BlockSpec(memory_space=pl.ANY),
        scratch_shapes=[
            pltpu.VMEM(bold.shape, bf16),
            pltpu.VMEM((2, windows, frames, sy, sz), bf16),
            pltpu.VMEM((windows, frames, sy, sz), bf16),
            pltpu.VMEM((voxels, count), bf16),
            pltpu.VMEM((sx, frames * sy, sz), f32),
            pltpu.VMEM((windows, sx, frames, sz), f32),
            pltpu.VMEM((windows, sx, frames, sz), f32),
            pltpu.VMEM((frames, voxels), bf16),
            pltpu.VMEM((windows, blocks, frames, block_rows), bf16),
            pltpu.SemaphoreType.DMA,
            pltpu.SemaphoreType.DMA((windows, 3)),
            pltpu.SemaphoreType.DMA((windows, 3)),
            pltpu.SemaphoreType.DMA((windows,)),
            pltpu.SemaphoreType.DMA((windows,)),
            pltpu.SemaphoreType.DMA((windows,)),
            pltpu.SemaphoreType.DMA((windows, 9)),
            pltpu.SemaphoreType.DMA((windows, slabs)),
        ],
        compiler_params=pltpu.CompilerParams(
            collective_id=0, has_side_effects=True, vmem_limit_bytes=40 * 1024 * 1024
        ),
        name="panels",
    )(gm_index.reshape(1, count), bold)
    return pl.pallas_call(
        functools.partial(tile_kernel, rows, cols),
        out_shape=jax.ShapeDtypeStruct((blocks, slots, windows, block_rows, block_rows), bf16),
        grid_spec=pltpu.PrefetchScalarGridSpec(
            num_scalar_prefetch=1,
            grid=(blocks,),
            in_specs=[pl.BlockSpec(memory_space=pltpu.VMEM)],
            out_specs=pl.BlockSpec(
                (1, slots, windows, block_rows, block_rows), lambda i, names: (i, 0, 0, 0, 0)
            ),
        ),
        compiler_params=pltpu.CompilerParams(vmem_limit_bytes=40 * 1024 * 1024),
        name="tiles",
    )(partners, cand)


def solution(mesh):
    rows, cols = mesh.shape["row"], mesh.shape["col"]
    in_specs = (P("subj", None, "row", "col", None), P(("row", "col")), P(("row", "col"), None))
    out_specs = P(("row", "col"), None, "subj", None, None)
    return jax.shard_map(
        functools.partial(on_device, rows, cols),
        mesh=mesh,
        in_specs=in_specs,
        out_specs=out_specs,
        check_vma=False,
    )
```
